32 devices in a mesh: grp: 4 (over y, core), dev: 8 (over z, x).
Axes of the slice: x: 2, y: 2, z: 4, core: 2. Of those that a mesh axis runs over, the one named last changes fastest.
Arguments:
- train_grads: bfloat16 [4096, 1024], P(('grp', 'dev')), may hold values from -192 to 192, as said below
- queries: bfloat16 [512, 1024], P('grp'), may hold values from -6 to 6
Outputs:
- scores: bfloat16 [4096, 512], P(('grp', 'dev'))
The draws below stay inside these ranges and needn't reach their ends.
Inputs may be any that keep to these rules, and one draw needn't show every extreme that they name: `train_grads`: Real-valued projected gradients whose columns and rows differ in scale.
All inputs are finite; a program needn't handle non-finite values. Where the reference program divides by a largest or mean magnitude, that divisor is 1e-20 or more.
Results may differ from the reference program's by a relative error of at most 0.001.
The reference program's roundings to bfloat16 on the way (of `prepared`) count: a program that leaves them out, or rounds other values in their place, can miss the bound.
Values may be sent and summed in bfloat16 or wider, within the bound.
No kernel may reach another device: no remote copies, remote signals or barrier semaphores. Data moves between devices by JAX's collectives and lax.ppermute only.
A program may use at most 64 MiB of HBM per device.

```python
import jax
import jax.numpy as jnp
from jax import lax

K = 1024
ROWS_DEV = 128
ITERS = 8
TOTAL = 4096
QTOT = 512
N_GRP = 4
N_DEV = 8


def draw_train_grads(key, part):
    key_cols = jax.random.fold_in(key, 11)
    key_perm = jax.random.fold_in(key, 12)
    key_base = jax.random.fold_in(key, 13)
    colscale = jnp.exp(jax.random.uniform(key_cols, (K,), jnp.float32, 0.0, jnp.log(10.0)))
    order = jax.random.permutation(key_perm, K)
    position = jnp.arange(TOTAL, dtype=jnp.float32) / TOTAL
    rowscale = jnp.exp(jnp.log(3.0) * position)
    base = jnp.clip(jax.random.normal(key_base, (TOTAL, K), jnp.float32), -4.0, 4.0)
    mixed = base + 0.6 * base[:, order]
    return (mixed * colscale[None, :] * rowscale[:, None]).astype(jnp.bfloat16)


def block_levels(own_key, shape, pieces, low, top_value):
    def one(dim, blocks):
        draws = jax.random.uniform(jax.random.fold_in(jax.random.fold_in(own_key, 6), dim), (blocks,), jnp.float32, low / len(pieces), top_value / len(pieces))
        return jnp.repeat(jnp.exp(draws), shape[dim] // blocks).reshape((-1,) + (1,) * (len(shape) - dim - 1))

    gain = one(*pieces[0])
    for cut in pieces[1:]:
        gain = gain * one(*cut)
    return gain


def centred(rng, extent, width, most, pieces=(), held_as=jnp.bfloat16):
    loudness = block_levels(rng, extent, pieces, -0.22, 0.18) if pieces else 1.0
    drawn = jax.random.normal(rng, extent, jnp.float32) * width * loudness
    return jnp.minimum(jnp.maximum(drawn, -most), most).astype(held_as)


def setup_inputs(seed: int = 0) -> dict:
    arg_keys = jax.random.split(jax.random.key(seed), 3)
    return {
        "train_grads": draw_train_grads(jax.random.fold_in(arg_keys[2], 71), 0),
        "queries": centred(arg_keys[1], (QTOT, K), 1.0, 6.0, ((0, 4),)),
    }


damping_ratio = 0.1


def reference(train_grads, queries):
    gram = lax.dot_general(train_grads, train_grads, (((0,), (0,)), ((), ())), preferred_element_type=jnp.float32)
    normed = gram / TOTAL
    mean_eig = jnp.trace(gram) / (TOTAL * K)
    damp = damping_ratio * mean_eig
    bound = jnp.max(jnp.sum(jnp.abs(normed), axis=1)) + damp
    step = 1.0 / bound
    oper = normed + damp * jnp.eye(K, dtype=jnp.float32)
    qvals = queries.astype(jnp.float32)
    state = step * qvals
    for index in range(ITERS):
        state = state + step * (qvals - jnp.dot(state, oper, precision=lax.Precision.HIGHEST))
    prepared = state.astype(jnp.bfloat16)
    blocks = train_grads.reshape(N_GRP * N_DEV, ROWS_DEV, K)

    def one_block(rows_block):
        return lax.dot_general(rows_block, prepared, (((1,), (1,)), ((), ())), preferred_element_type=jnp.float32).astype(jnp.bfloat16)

    return lax.map(one_block, blocks).reshape(TOTAL, QTOT)
```

```python
import functools
import itertools

import jax
import jax.numpy as jnp
from jax import lax
from jax.experimental import pallas as pl
from jax.experimental.pallas import tpu as pltpu
from jax.sharding import PartitionSpec as P

ITERS = 8
TILE = 128
AXES = ("grp", "dev")
GATHER_LIMIT = 8 << 20

damping_ratio = 0.1


def tri(count):
    return [(i, j) for i in range(count) for j in range(i, count)]


def load_all(refs, dest, sems):
    rows = refs[0].shape[0]
    copies = [
        pltpu.make_async_copy(ref, dest.at[pl.ds(k * rows, rows)], sems.at[k])
        for k, ref in enumerate(refs)
    ]
    for copy in copies:
        copy.start()
    for copy in copies:
        copy.wait()


def row_products(held, i):
    return lax.dot_general(
        held[:, i * TILE : (i + 1) * TILE],
        held[:, i * TILE :],
        (((0,), (0,)), ((), ())),
        preferred_element_type=jnp.float32,
    )


def gram_kernel(count, has_base, *refs):
    blocks, refs = refs[:count], refs[count:]
    base = refs[0] if has_base else None
    out, held, sems = refs[-3:]
    load_all(blocks, held, sems)
    tiles = held.shape[1] // TILE
    for i in range(tiles):
        product = row_products(held, i)
        first = i * tiles - i * (i - 1) // 2
        for j in range(i, tiles):
            part = product[:, (j - i) * TILE : (j - i + 1) * TILE]
            out[first + j - i] = part + base[first + j - i] if has_base else part


def gram_of(blocks, base=None):
    rows, width = blocks[0].shape
    shape = jax.ShapeDtypeStruct((len(tri(width // TILE)), TILE, TILE), jnp.float32)
    args = list(blocks) + ([] if base is None else [base])
    depth = rows * len(blocks)
    return pl.pallas_call(
        functools.partial(gram_kernel, len(blocks), base is not None),
        out_shape=shape,
        in_specs=[pl.BlockSpec(memory_space=pl.ANY)] * len(blocks)
        + ([] if base is None else [pl.BlockSpec(memory_space=pltpu.VMEM)]),
        out_specs=pl.BlockSpec(memory_space=pltpu.VMEM),
        scratch_shapes=[
            pltpu.VMEM((depth, width), blocks[0].dtype),
            pltpu.SemaphoreType.DMA((len(blocks),)),
        ],
        cost_estimate=pl.CostEstimate(
            flops=depth * width * width, bytes_accessed=2 * depth * width, transcendentals=0
        ),
        compiler_params=pltpu.CompilerParams(vmem_limit_bytes=40 << 20),
    )(*args)


def solve_kernel(n_sums, n_late, n_rows, total, *refs):
    sums, refs = refs[:n_sums], refs[n_sums:]
    late, refs = refs[:n_late], refs[n_late:]
    rows, refs = refs[:n_rows], refs[n_rows:]
    queries, refs = refs[0], refs[1:]
    outs, refs = refs[:n_rows], refs[n_rows:]
    high, low, spread, held, sems = refs
    width = queries.shape[1]
    tiles = width // TILE
    if n_late:
        load_all(late, held, sems)
    spread[...] = jnp.zeros_like(spread)
    diagonal = jnp.zeros((TILE, TILE), jnp.float32)
    on_diagonal = lax.broadcasted_iota(jnp.int32, (TILE, TILE), 0) == lax.broadcasted_iota(
        jnp.int32, (TILE, TILE), 1
    )

    def place(value, i, j):
        at = (slice(i * TILE, (i + 1) * TILE), slice(j * TILE, (j + 1) * TILE))
        top = value.astype(jnp.bfloat16)
        high[at] = top
        low[at] = (value - top.astype(jnp.float32)).astype(jnp.bfloat16)
        spread[at[0]] += jnp.abs(value)

    for i in range(tiles):
        product = row_products(held, i) if n_late else None
        first = i * tiles - i * (i - 1) // 2
        for j in range(i, tiles):
            value = functools.reduce(jnp.add, [s[first + j - i] for s in sums])
            if n_late:
                value = value + product[:, (j - i) * TILE : (j - i + 1) * TILE]
            place(value, i, j)
            if i == j:
                diagonal = diagonal + jnp.where(on_diagonal, value, 0.0)
            else:
                place(value.T, j, i)

    damp = damping_ratio * jnp.sum(diagonal) / (total * width)
    bound = jnp.max(jnp.sum(spread[...], axis=1, keepdims=True)) / total + damp
    step = 1.0 / bound
    scale = step / total
    keep = 1.0 - step * damp
    start = step * queries[...].astype(jnp.float32)

    def advance(_, state):
        top = state.astype(jnp.bfloat16)
        rest = (state - top.astype(jnp.float32)).astype(jnp.bfloat16)
        moved = jnp.dot(top, high[...], preferred_element_type=jnp.float32)
        moved = moved + jnp.dot(rest, high[...], preferred_element_type=jnp.float32)
        moved = moved + jnp.dot(top, low[...], preferred_element_type=jnp.float32)
        return start + (keep * state - scale * moved)

    prepared = lax.fori_loop(0, ITERS, advance, start).astype(jnp.bfloat16)
    for block, out in zip(rows, outs, strict=True):
        out[...] = lax.dot_general(
            block[...], prepared, (((1,), (1,)), ((), ())), preferred_element_type=jnp.float32
        ).astype(jnp.bfloat16)


def solve_and_score(sums, late, rows, queries, total):
    count, width = queries.shape
    depth = sum(block.shape[0] for block in late)
    return pl.pallas_call(
        functools.partial(solve_kernel, len(sums), len(late), len(rows), total),
        out_shape=[jax.ShapeDtypeStruct((block.shape[0], count), jnp.bfloat16) for block in rows],
        in_specs=[pl.BlockSpec(memory_space=pltpu.VMEM)] * len(sums)
        + [pl.BlockSpec(memory_space=pl.ANY)] * len(late)
        + [pl.BlockSpec(memory_space=pltpu.VMEM)] * (len(rows) + 1),
        out_specs=[pl.BlockSpec(memory_space=pltpu.VMEM)] * len(rows),
        scratch_shapes=[
            pltpu.VMEM((width, width), jnp.bfloat16),
            pltpu.VMEM((width, width), jnp.bfloat16),
            pltpu.VMEM((width, TILE), jnp.float32),
            pltpu.VMEM((max(depth, 16), width), jnp.bfloat16),
            pltpu.SemaphoreType.DMA((max(len(late), 1),)),
        ],
        cost_estimate=pl.CostEstimate(
            flops=6 * ITERS * count * width * width, bytes_accessed=4 * width * width, transcendentals=0
        ),
        compiler_params=pltpu.CompilerParams(vmem_limit_bytes=56 << 20),
    )(*sums, *late, *rows, queries)


def lay_kernel(count, where, *refs):
    blocks, out = refs[:count], refs[count]
    wide = blocks[0].shape[1]
    for k, block in enumerate(blocks):
        at = pl.multiple_of((where[0] ^ k) * wide, wide)
        out[:, pl.ds(at, wide)] = block[...]


def lay_out(blocks, index):
    rows, wide = blocks[0].shape
    return pl.pallas_call(
        functools.partial(lay_kernel, len(blocks)),
        out_shape=jax.ShapeDtypeStruct((rows, wide * len(blocks)), blocks[0].dtype),
        in_specs=[pl.BlockSpec(memory_space=pltpu.SMEM)]
        + [pl.BlockSpec(memory_space=pltpu.VMEM)] * len(blocks),
        out_specs=pl.BlockSpec(memory_space=pltpu.VMEM),
    )(jnp.reshape(index, (1,)).astype(jnp.int32), *blocks)


def flip(value, shape, grp_bits, dev_bits):
    n_grp, n_dev = shape
    pairs = [
        (g * n_dev + d, (g ^ grp_bits) * n_dev + (d ^ dev_bits))
        for g in range(n_grp)
        for d in range(n_dev)
    ]
    return lax.ppermute(value, AXES, pairs)


def power_of_two(value):
    return value > 0 and value & (value - 1) == 0


def routes(n_grp, n_dev):
    far = (0, n_dev // 2)
    near = [(0, 1 << k) for k in range(n_dev.bit_length() - 2)]
    near += [(1 << k, 0) for k in range(1, n_grp.bit_length() - 1)]
    near = near[:1] + near[:0:-1]
    load = {way: 2 + (way[1] == n_dev // 4) for way in near}
    found = [(far, far)] + [(way, way) for way in near]
    with_far = [((way[0] ^ far[0], way[1] ^ far[1]), way) for way in near]
    for size in range(2, len(near) + 1):
        groups = list(itertools.combinations(near, size))
        for extra in ((0, 0), far):
            for group in groups:
                offset = extra
                for way in group:
                    offset = (offset[0] ^ way[0], offset[1] ^ way[1])
                way = min(group, key=load.get)
                load[way] += 1
                found.append((offset, way))
            if size == 2 and not any(extra):
                found += with_far
    return found


def gathered_body(shape, train_grads, queries):
    n_grp, n_dev = shape
    total = train_grads.shape[0] * n_grp * n_dev
    swap = functools.partial(flip, shape=shape)

    def across(block):
        return swap(block, grp_bits=1, dev_bits=0)

    held = {(0, 0): train_grads}
    for offset, way in routes(n_grp, n_dev):
        source = held[offset[0] ^ way[0], offset[1] ^ way[1]]
        held[offset] = swap(source, grp_bits=way[0], dev_bits=way[1])
    blocks = list(held.values())
    half = (len(blocks) - 1) // 2
    first = gram_of(blocks[:half])
    mine = gram_of(blocks[half:-3], first)
    other = across(mine)
    last = blocks[-3:]
    last = last + [across(block) for block in last]
    rows = [
        across(held[k - 1, 0]) if k % 2 else held[k, 0] for k in range(n_grp)
    ]
    scores = solve_and_score([mine, other], last, rows, queries, total)
    moved = [scores[0]] + [
        swap(part, grp_bits=k, dev_bits=0) for k, part in enumerate(scores) if k
    ]
    return lay_out(moved, lax.axis_index("grp"))


def summed_body(shape, train_grads, queries):
    n_grp, n_dev = shape
    total = train_grads.shape[0] * n_grp * n_dev
    gram = lax.psum(gram_of([train_grads]), AXES)
    eye = jnp.eye(queries.shape[1], dtype=jnp.bfloat16)
    (prepared,) = solve_and_score([gram], [], [eye], queries, total)
    return lax.dot_general(
        train_grads,
        lax.all_gather(prepared, "grp", axis=1, tiled=True),
        (((1,), (0,)), ((), ())),
        preferred_element_type=jnp.float32,
    ).astype(jnp.bfloat16)


def solution(mesh):
    shape = (mesh.shape["grp"], mesh.shape["dev"])

    def body(train_grads, queries):
        rows, width = train_grads.shape
        held = rows * width * 2 * shape[0] * shape[1]
        fits = held <= GATHER_LIMIT and all(power_of_two(n) and n > 2 for n in shape)
        return (gathered_body if fits else summed_body)(shape, train_grads, queries)

    return jax.shard_map(
        body,
        mesh=mesh,
        in_specs=(P(("grp", "dev"), None), P("grp", None)),
        out_specs=P(("grp", "dev"), None),
        check_vma=False,
    )
```
